128 devices in a mesh: dp: 8 (over z, core), group: 16 (over y, x).
Axes of the slice: x: 4, y: 4, z: 4, core: 2. Of those that a mesh axis runs over, the one named last changes fastest.
Arguments:
- points: bfloat16 [1048576, 1024], P(('dp', 'group')), may hold values from -12 to 12
- block_rows: int32 [8192], P(('dp', 'group')), may hold values from 1 to 128
- block_owner: int32 [8192, 1], P(('dp', 'group')), may hold values from 0 to 127; in each aligned block of 64 rows (0 to 63, 64 to 127, ...) at most 2 rows name the same one
- block_local: int32 [8192], P(('dp', 'group')), may hold values from 0 to 7
- assign_mid: int32 [1024, 1], P(('dp', 'group')), may hold values from 0 to 511
- assign_top: int32 [512, 1], P('group'), may hold values from 0 to 255
Outputs:
- level1: float32 [1024, 1024], P(('dp', 'group'))
- best: float32 [1048576], P(('dp', 'group'))
- level2: float32 [512, 1024], P('group')
- level3: float32 [256, 1024], replicated
The draws below stay inside these ranges and needn't reach their ends.
Inputs may be any that keep to these rules, and one draw needn't show every extreme that they name: `block_owner`: among the blocks of one device, no owner is named more than 2 times. `assign_mid`: every level-2 cluster is named by at least one level-1 centroid. `assign_top`: every level-3 cluster is named by at least one level-2 centroid.
All inputs are finite; a program needn't handle non-finite values.
Results may differ from the reference program's by a relative error of at most 0.0014.
Values may be sent and summed in bfloat16 or wider, within the bound.
A program may use at most 64 MiB of HBM per device.

```python
import math
import jax
import jax.numpy as jnp
import numpy as np
from jax import lax

D = 1024
BLOCK = 128
SLOTS = 2
P_DEV = 8192
K1_DEV = 8
K3 = 256
K1 = 1024
K2 = 512
POINTS = 1048576
BLOCKS = 8192
DEVICES = 128


def place_ends(result, stream_key, least, top_value):
    index_at = [jax.random.randint(jax.random.fold_in(stream_key, axis), (), 0, length) for axis, length in enumerate(result.shape)]
    widest = result.shape.index(max(result.shape))
    neighbour = index_at[:widest] + [(index_at[widest] + 1) % result.shape[widest]] + index_at[widest + 1:]
    return result.at[tuple(index_at)].set(least).at[tuple(neighbour)].set(top_value)


def block_levels(stream_key, shape, pieces, low, top_value):
    level, own = 1.0, jax.random.fold_in(stream_key, 6)
    for dim, parts in pieces:
        draws = jnp.exp(jax.random.uniform(jax.random.fold_in(own, dim), (parts,), jnp.float32, low / len(pieces), top_value / len(pieces)))
        level = level * jnp.repeat(draws, shape[dim] // parts).reshape([-1 if axis == dim else 1 for axis in range(len(shape))])
    return level


def picks_of(own_key, rows, count, top, lift):
    sequence = jax.random.permutation(jax.random.fold_in(own_key, 1), count)
    favour = sequence
    for power in range(3):
        favour = favour * favour // count
    favour = favour * lift // count
    lots = jax.random.randint(jax.random.fold_in(own_key, 2), (rows, count), 0, 4096) + favour
    fixed_rows = jax.random.permutation(jax.random.fold_in(own_key, 3), rows)[jnp.arange(count) % rows]
    lots = jnp.where(jnp.arange(rows)[:, None] == fixed_rows[None, :], 1 << 14, lots)
    score = lots * count + jnp.arange(count)
    return lax.top_k(score.astype(jnp.int32), top)[1].astype(jnp.int32)


def assign_block(own_key, own, number, rows, number_of, top, most, slope):
    sequence = jax.random.permutation(own_key, number_of)
    packed, usual = shares(number_of, rows * top, most, slope, True), shares(number_of, rows * top, most, slope, False)
    places = jnp.arange(number_of)

    def named(sizes, offset_by):
        used = int((sizes > 0).sum())
        fixed = max(1, used // 4)
        moved = fixed + (places - fixed + offset_by * (used - fixed)) % max(1, number_of - fixed)
        return jnp.zeros((number_of,), jnp.int32).at[sequence[jnp.where(places < fixed, places, moved)]].set(jnp.asarray(sizes, jnp.int32))

    sizes = jnp.where(number % 4 == 0, named(packed, number // 4), named(usual, number - number // 4 - 1))
    mixed = jax.random.permutation(jax.random.fold_in(own, 3), number_of)
    source_of, taker = mixed[0:number_of // 2 * 2:2], mixed[1:number_of // 2 * 2:2]
    slack = jnp.minimum(sizes[source_of] - 1, most - sizes[taker]) // 2
    slack = jnp.where((source_of == sequence[0]) | (taker == sequence[0]) | (sizes[taker] == 0), 0, jnp.maximum(slack, 0))
    moved = jax.random.randint(jax.random.fold_in(own, 4), (number_of // 2,), 0, 1 << 20) % (slack + 1)
    sizes = sizes.at[source_of].add(-moved).at[taker].add(moved)
    labels = jnp.searchsorted(jnp.cumsum(sizes), jnp.arange(rows * top), side="right").astype(jnp.int32)
    grid = labels.reshape(top, rows).T
    grid = grid[jax.random.permutation(jax.random.fold_in(own, 1), rows)]
    offset_by = jax.random.randint(jax.random.fold_in(own, 2), (rows, 1), 0, top)
    return jnp.take_along_axis(grid, (jnp.arange(top)[None, :] + offset_by) % top, axis=1)


def shares(count, total, limit, lean, full):
    loads = [(1 << 20) // math.isqrt(grade ** lean) + 1 for grade in range(1, count + 1)]
    largest = limit if full else min(limit, max(-(-total // count), total * loads[0] // sum(loads)))
    least = 1 if total - largest >= count - 1 else 0
    counts, spare = [largest] + [least] * (count - 1), total - largest - least * (count - 1)
    while spare > 0:
        movable = [i for i in range(1, count) if counts[i] < largest] or [i for i in range(1, count) if counts[i] < limit]
        mass, remaining = sum([loads[i] for i in movable]), spare
        for i in movable:
            extra = min(limit - counts[i], max(1, remaining * loads[i] // mass), spare)
            counts[i] = counts[i] + extra
            spare = spare - extra
    return np.array(counts)


def noise(stream_key, extent, scale, reach, pieces=(), kind=jnp.bfloat16):
    result = jax.random.normal(stream_key, extent, jnp.float32) * scale
    if len(pieces) > 0:
        result = block_levels(stream_key, extent, pieces, -0.22, 0.18) * result
    return jnp.clip(result, min=-reach, max=reach).astype(kind)


def setup_inputs(seed: int = 0) -> dict:
    key_list = jax.random.split(jax.random.key(seed), 7)
    points = noise(key_list[0], (POINTS, D), 2.0, 12.0, ((0, 128),))
    block_rows = place_ends(jax.random.randint(key_list[1], (BLOCKS,), 1, BLOCK + 1), jax.random.fold_in(key_list[1], 1), 1, BLOCK).astype(jnp.int32)
    block_owner_keys = jax.random.split(jax.random.fold_in(key_list[2], 1), BLOCKS // (P_DEV // BLOCK))
    block_owner_turns = jax.random.permutation(jax.random.fold_in(key_list[2], 3), BLOCKS // (P_DEV // BLOCK))
    block_owner = jax.vmap(lambda own, number: assign_block(jax.random.fold_in(key_list[2], 2), own, number, P_DEV // BLOCK, DEVICES, 1, SLOTS, 2))(block_owner_keys, block_owner_turns).reshape((BLOCKS, 1))
    block_local = place_ends(jax.random.randint(key_list[3], (BLOCKS,), 0, K1_DEV), jax.random.fold_in(key_list[3], 1), 0, K1_DEV - 1).astype(jnp.int32)
    assign_mid = picks_of(key_list[4], K1, K2, 1, 0)
    assign_top = picks_of(key_list[5], K2, K3, 1, 0)
    return dict(points=points, block_rows=block_rows, block_owner=block_owner, block_local=block_local, assign_mid=assign_mid, assign_top=assign_top)


def reference(points, block_rows, block_owner, block_local, assign_mid, assign_top):
    feature_width = points.shape[1]
    block_count = P_DEV // BLOCK
    position = lax.broadcasted_iota(jnp.int32, (DEVICES, block_count, BLOCK), 2)
    live_rows = (position < block_rows.reshape(DEVICES, block_count, 1)).astype(jnp.float32)
    grouped = points.reshape(DEVICES, block_count, BLOCK, feature_width)

    def block_total(pair):
        masks, values = pair
        return jnp.einsum("bp,bpd->bd", masks, values.astype(jnp.float32))

    block_sums = lax.map(block_total, (live_rows, grouped)).reshape(DEVICES * block_count, feature_width)
    cluster = (block_owner[:, 0] * K1_DEV + block_local).astype(jnp.int32)
    level1_sums = jax.ops.segment_sum(block_sums, cluster, num_segments=K1)
    level1_counts = jax.ops.segment_sum(block_rows.astype(jnp.float32), cluster, num_segments=K1)
    level1 = level1_sums / jnp.maximum(level1_counts, 1.0)[:, None]
    rounded = level1.astype(jnp.bfloat16)
    widened = rounded.astype(jnp.float32)
    half_norm = 0.5 * jnp.sum(widened * widened, axis=1)
    live_points = live_rows.reshape(DEVICES, P_DEV)
    shard_points = points.reshape(DEVICES, P_DEV, feature_width)

    def scoring(pair):
        values, masks = pair
        product = jnp.dot(values, rounded.T, preferred_element_type=jnp.float32)
        return jnp.max(product - half_norm[None, :], axis=1) * masks

    best = lax.map(scoring, (shard_points, live_points)).reshape(DEVICES * P_DEV)
    mid_ids = assign_mid[:, 0].astype(jnp.int32)
    mid_counts = jax.ops.segment_sum(jnp.ones((K1,), jnp.float32), mid_ids, num_segments=K2)
    level2 = jax.ops.segment_sum(level1, mid_ids, num_segments=K2) / mid_counts[:, None]
    top_ids = assign_top[:, 0].astype(jnp.int32)
    top_counts = jax.ops.segment_sum(jnp.ones((K2,), jnp.float32), top_ids, num_segments=K3)
    level3 = jax.ops.segment_sum(level2, top_ids, num_segments=K3) / top_counts[:, None]
    return (level1, best, level2, level3)
```

```python
import functools

import jax
import jax.numpy as jnp
from jax import lax
from jax.experimental import pallas as pl
from jax.experimental.pallas import tpu as pltpu
from jax.sharding import PartitionSpec as P

MESH = pl.DeviceIdType.MESH
F32 = jnp.float32
BF16 = jnp.bfloat16
I32 = jnp.int32

D = 1024
NB = 64
NP = 8192
ND = 128
K1 = 1024
TM = 512
CH = 4
NT = (((1,), (1,)), ((), ()))


def wait_for(ref, sem):
    pltpu.make_async_copy(ref, ref, sem).wait()


def iota(shape, dim):
    return lax.broadcasted_iota(I32, shape, dim)


def split2(v):
    hi = v.astype(BF16)
    return hi, (v - hi.astype(F32)).astype(BF16)


def kernel(
    pts, rows_s, own_s, loc_s, mid_s, top_s,
    lvl1, best, lvl2, lvl3,
    xbuf, s2, sendb, recvb, msend, meta, pm, b8, amat, ot, cg, own_st, wb, wm, rmax, hn, wsel, dum15,
    xsem, bs_s, bs_r, m_s, m_r, r1, t1, r2, t2, r3, t3,
):
    dp, g = lax.axis_index("dp"), lax.axis_index("group")
    z, core, y, x = dp // 2, dp % 2, g // 4, g % 4
    me = dp * 16 + g

    def dev(zz, cc, yy, xx):
        return (zz * 2 + cc, yy * 4 + xx)

    def other(i):
        zz = (z + i // 32) % 4
        cc = (core + (i // 16) % 2) % 2
        yy = (y + (i // 4) % 4) % 4
        xx = (x + i % 4) % 4
        return zz, cc, yy, xx

    for j in range(8):
        pltpu.make_async_copy(pts.at[pl.ds(1024 * j, 1024)], xbuf.at[pl.ds(1024 * j, 1024)], xsem.at[j]).start()

    barrier = pltpu.get_barrier_semaphore()

    def greet(i, c):
        pl.semaphore_signal(barrier, inc=1, device_id=dev(*other(i)), device_id_type=MESH)
        return c

    lax.fori_loop(1, ND, greet, 0)

    lane1 = iota((1, 128), 1)
    m = jnp.zeros((1, 128), I32)
    for b in range(NB):
        m = jnp.where(lane1 == b, (own_s[b] * 8 + loc_s[b]) * 256 + rows_s[b], m)
    for i in range(8):
        m = jnp.where(lane1 == NB + i, mid_s[i], m)
    for i in range(32):
        m = jnp.where(lane1 == NB + 8 + i, top_s[i], m)
    msend[0] = m

    sub8 = iota((8, 1024), 0)
    lane8 = iota((8, 1024), 1)
    in_block = (lane8 // 128) == sub8
    pos = lane8 % 128

    def block_sums(j):
        wait_for(xbuf.at[pl.ds(1024 * j, 1024)], xsem.at[j])
        rv = jnp.zeros((8, 1024), I32)
        for r in range(8):
            rv = jnp.where(sub8 == r, rows_s[8 * j + r], rv)
        mask = jnp.where(in_block & (pos < rv), 1.0, 0.0).astype(BF16)
        s = jnp.dot(mask, xbuf[1024 * j : 1024 * (j + 1), :], preferred_element_type=F32)
        s2[8 * j : 8 * (j + 1), :] = s
        s2[NB + 8 * j : NB + 8 * (j + 1), :] = s

    for j in range(4):
        block_sums(j)

    pl.semaphore_wait(barrier, ND - 1)

    def send_meta(i, c):
        pltpu.make_async_remote_copy(
            src_ref=msend.at[0], dst_ref=meta.at[me], send_sem=m_s, recv_sem=m_r,
            device_id=dev(*other(i)), device_id_type=MESH,
        ).start()
        return c

    lax.fori_loop(1, ND, send_meta, 0)
    meta[me] = msend[0]

    for j in range(4, 8):
        block_sums(j)

    low = iota((16, 8, 128), 2) < 64
    for t in range(8):
        xt = jnp.transpose(s2[:, 128 * t : 128 * (t + 1)]).reshape(16, 8, 128)
        yt = pltpu.roll(xt, 4, 1)
        sendb[16 * t : 16 * (t + 1)] = jnp.where(low, xt, yt)[:, 0:4, :]

    def send_sums(i, c):
        zz, cc, yy, xx = other(i)
        pltpu.make_async_remote_copy(
            src_ref=sendb.at[zz * 32 + cc * 16 + yy * 4 + xx], dst_ref=recvb.at[me], send_sem=bs_s, recv_sem=bs_r,
            device_id=dev(zz, cc, yy, xx), device_id_type=MESH,
        ).start()
        return c

    lax.fori_loop(1, ND, send_sums, 0)
    recvb[me] = sendb[me]

    wait_for(meta.at[pl.ds(0, ND - 1)], m_r)
    mt = meta[...].reshape(ND, 128)
    lane64 = iota((64, 128), 1)
    paired = jnp.where(lane64 < 64, mt[0:64], pltpu.roll(mt[64:128], 64, 1))
    pm[0] = paired // 2048
    pm[1] = (paired // 256) % 8
    pm[2] = paired % 256
    sub128 = iota((128, 128), 0)

    def owners(p, c):
        k = pl.ds(pl.multiple_of(p * 128, 128), 128)
        ot[:, k] = jnp.where(sub128 == pm[0, pl.ds(p, 1), :], 1.0, 0.0).astype(BF16)
        return c

    lax.fori_loop(0, 64, owners, 0)

    metat = jnp.transpose(mt.astype(F32))
    am = [metat[NB + l : NB + l + 1, :].astype(I32) for l in range(8)]
    am = jnp.concatenate(am, axis=1)
    gof, iof = am // 32, am % 32
    gsel = jnp.where(iota((128, K1), 0) == gof, 1.0, 0.0).astype(BF16)
    isel = jnp.where(iota((32, K1), 0) == iof, 1.0, 0.0)
    n_mid = lax.dot_general(isel.astype(BF16), gsel, NT, preferred_element_type=F32)
    lane32 = iota((32, 128), 1)
    own_n = jnp.sum(jnp.where(lane32 == g, n_mid, 0.0), axis=1, keepdims=True)
    tops = metat[NB + 8 : NB + 40, :]
    inv = 1.0 / jnp.maximum(n_mid, 1.0)
    ih, im = split2(inv)
    table = jnp.concatenate([ih, im, tops.astype(BF16)], axis=0)
    looked = jnp.dot(table, gsel, preferred_element_type=F32)
    inv_c = jnp.sum((looked[0:32] + looked[32:64]) * isel, axis=0, keepdims=True)
    top_c = jnp.sum(looked[64:96] * isel, axis=0, keepdims=True).astype(I32)
    w3 = jnp.where(iota((256, K1), 0) == top_c, inv_c, 0.0)
    w3h, w3m = split2(w3)
    wsel[0:256] = w3h
    wsel[256:288] = jnp.where(iota((32, K1), 0) + 32 * g == am, 1.0, 0.0).astype(BF16)
    lane16, sub16 = iota((16, K1), 1), iota((16, K1), 0)
    wsel[288:304] = jnp.where((lane16 == sub16 * 128 + me) & (sub16 < 8), 1.0, 0.0).astype(BF16)
    wsel[304:560] = w3m
    sub256 = iota((256, 128), 0)
    n_top = jnp.zeros((256, 128), F32)
    for i in range(32):
        n_top = n_top + jnp.where(sub256 == tops[i : i + 1, :].astype(I32), 1.0, 0.0)
    n_top = jnp.sum(jnp.where(iota((256, 128), 1) < 16, n_top, 0.0), axis=1, keepdims=True)

    wait_for(recvb.at[pl.ds(0, ND - 1)], bs_r)
    low4 = iota((4, 128), 1) < 64
    sub16b = iota((16, 128), 0)

    def left(p, c):
        k = pl.ds(pl.multiple_of(p * 128, 128), 128)
        a, b = recvb[p], recvb[p + 64]
        b8[0:4, :] = jnp.where(low4, a, pltpu.roll(b, 64, 1))
        b8[4:8, :] = jnp.where(low4, pltpu.roll(a, 64, 1), b)
        v = b8[...]
        hi, mid = split2(v)
        hm = jnp.concatenate([hi.astype(F32), mid.astype(F32)], axis=0)
        loc = pm[1, pl.ds(p, 1), :]
        for l in range(8):
            amat[16 * l : 16 * (l + 1), k] = jnp.where(loc == l, hm, 0.0).astype(BF16)
        cnt = pm[2, pl.ds(p, 1), :].astype(F32)
        amat[128:144, k] = jnp.where(sub16b == loc, cnt, 0.0).astype(BF16)
        return c

    lax.fori_loop(0, 64, left, 0)

    def cluster_sums(k, acc):
        ks = pl.ds(pl.multiple_of(k * 1024, 1024), 1024)
        return acc + lax.dot_general(amat[:, ks], ot[:, ks], NT, preferred_element_type=F32)

    sums = lax.fori_loop(0, 8, cluster_sums, jnp.zeros((144, 128), F32))
    for l in range(8):
        c1 = (sums[16 * l : 16 * l + 8] + sums[16 * l + 8 : 16 * l + 16]) / jnp.maximum(sums[128 + l : 129 + l], 1.0)
        hi, mid = split2(c1)
        own_st[l] = hi
        own_st[8 + l] = mid

    def slab(ch, zz, cc, yy, xx):
        return cg.at[pl.ds(2 * ch, 2), zz, cc, yy, xx]

    everything = slice(None)

    def forms(ch):
        if ch % 3 == 0:
            return (
                lambda a, b: (z, core, (y + a) % 4, (x + b) % 4),
                (z, core, everything, everything),
                lambda d: ((z + d) % 4, core, y, x),
                lambda d: ((z + d) % 4, core, everything, everything),
            )
        if ch % 3 == 1:
            return (
                lambda a, b: ((z + a) % 4, core, (y + b) % 4, x),
                (everything, core, everything, x),
                lambda d: (z, core, y, (x + d) % 4),
                lambda d: (everything, core, everything, (x + d) % 4),
            )
        return (
            lambda a, b: ((z + a) % 4, core, y, (x + b) % 4),
            (everything, core, y, everything),
            lambda d: (z, core, (y + d) % 4, x),
            lambda d: (everything, core, (y + d) % 4, everything),
        )

    def hop1(ch):
        peer = forms(ch)[0]
        src = own_st.at[pl.ds(2 * ch, 2)]
        mine = slab(ch, z, core, y, x)
        pltpu.make_async_copy(src, mine, r1.at[ch]).start()

        def go(i, c):
            pltpu.make_async_remote_copy(
                src_ref=src, dst_ref=mine, send_sem=t1.at[ch], recv_sem=r1.at[ch],
                device_id=dev(*peer(i // 4, i % 4)), device_id_type=MESH,
            ).start()
            return c

        lax.fori_loop(1, 16, go, 0)

    def hop2(ch):
        _, part, peer, _ = forms(ch)
        ref = slab(ch, *part)
        wait_for(ref, r1.at[ch])
        for d in range(1, 4):
            pltpu.make_async_remote_copy(
                src_ref=ref, dst_ref=ref, send_sem=t2.at[ch, d - 1], recv_sem=r2.at[ch, d - 1],
                device_id=dev(*peer(d)), device_id_type=MESH,
            ).start()

    def hop3(ch):
        part = forms(ch)[3]
        for d in range(1, 4):
            wait_for(slab(ch, *part(4 - d)), r2.at[ch, d - 1])
        ref = slab(ch, everything, core, everything, everything)
        pltpu.make_async_remote_copy(
            src_ref=ref, dst_ref=ref, send_sem=t3.at[ch], recv_sem=r3.at[ch],
            device_id=dev(z, 1 - core, y, x), device_id_type=MESH,
        ).start()

    def arrive(ch):
        wait_for(slab(ch, everything, 1 - core, everything, everything), r3.at[ch])
        dst = wb if ch < CH else wm
        q = ch % CH
        for half in range(2):
            lanes = slice(256 * q + 128 * half, 256 * q + 128 * half + 128)
            sq = jnp.zeros((8, 128), F32)
            for zz in range(4):
                v = cg[2 * ch + half, zz].astype(F32).reshape(256, 128)
                dst[256 * zz : 256 * (zz + 1), lanes] = v.astype(BF16)
                if ch < CH:
                    sq = sq + jnp.sum((v * v).reshape(32, 8, 128), axis=0)
            if ch < CH:
                hn[:, lanes] = 0.5 * jnp.sum(sq, axis=0, keepdims=True)

    def drain(ch):
        wait_for(dum15, t1.at[ch])
        _, part, _, _ = forms(ch)
        for d in range(1, 4):
            wait_for(slab(ch, *part), t2.at[ch, d - 1])
        wait_for(slab(ch, everything, core, everything, everything), t3.at[ch])

    def scores(q, lo, hi):
        lanes = slice(256 * q, 256 * (q + 1))

        def tile(t, c):
            rs = pl.ds(pl.multiple_of(t * TM, TM), TM)
            p = jnp.dot(xbuf[rs, :], wb[:, lanes], preferred_element_type=F32) - hn[:, lanes]
            top = jnp.maximum(p[:, 0:128], p[:, 128:256])
            if q > 0:
                top = jnp.maximum(top, rmax[rs, :])
            rmax[rs, :] = top
            return c

        lax.fori_loop(lo, hi, tile, 0)

    hop1(0)
    hop1(1)
    hop2(0)
    hop1(2)
    hop2(1)
    hop3(0)
    hop1(3)
    hop2(2)
    hop3(1)
    arrive(0)
    n = NP // TM // 4
    scores(0, 0, n)
    hop2(3)
    hop3(2)
    scores(0, n, 2 * n)
    hop3(3)
    arrive(1)
    hop1(4)
    scores(0, 2 * n, 3 * n)
    hop2(4)
    hop1(5)
    scores(0, 3 * n, 4 * n)
    hop3(4)
    hop2(5)
    hop1(6)
    arrive(2)
    scores(1, 0, n)
    hop3(5)
    hop2(6)
    hop1(7)
    scores(1, n, 2 * n)
    hop3(6)
    hop2(7)
    scores(1, 2 * n, 3 * n)
    hop3(7)
    arrive(3)
    scores(1, 3 * n, 4 * n)
    scores(2, 0, 4 * n)
    scores(3, 0, 4 * n)

    def finish(b, c):
        v = jnp.transpose(rmax[pl.ds(pl.multiple_of(b * 128, 128), 128), :])
        row = jnp.max(v, axis=0, keepdims=True)
        best[pl.ds(b, 1), :] = jnp.where(lane1 < rows_s[b], row, 0.0 * row)
        return c

    lax.fori_loop(0, NB, finish, 0)

    for ch in range(CH, 2 * CH):
        arrive(ch)
    for d in range(4):
        ds = slice(256 * d, 256 * (d + 1))
        a = lax.dot_general(wsel[...], wb[ds, :], NT, preferred_element_type=F32)
        b = lax.dot_general(wsel[0:304, :], wm[ds, :], NT, preferred_element_type=F32)
        lvl3[:, ds] = (a[0:256] + a[304:560] + b[0:256]) / n_top
        lvl2[:, ds] = (a[256:288] + b[256:288]) / own_n
        lvl1[:, ds] = a[288:296] + b[288:296]

    wait_for(meta.at[pl.ds(0, ND - 1)], m_s)
    wait_for(recvb.at[pl.ds(0, ND - 1)], bs_s)
    for ch in range(2 * CH):
        drain(ch)


def local(points, block_rows, block_owner, block_local, assign_mid, assign_top):
    vmem = pl.BlockSpec(memory_space=pltpu.VMEM)
    smem = pl.BlockSpec(memory_space=pltpu.SMEM)
    lvl1, best, lvl2, lvl3 = pl.pallas_call(
        kernel,
        out_shape=(
            jax.ShapeDtypeStruct((8, D), F32),
            jax.ShapeDtypeStruct((NB, 128), F32),
            jax.ShapeDtypeStruct((32, D), F32),
            jax.ShapeDtypeStruct((256, D), F32),
        ),
        in_specs=[pl.BlockSpec(memory_space=pl.ANY)] + [smem] * 5,
        out_specs=(vmem, vmem, vmem, vmem),
        scratch_shapes=[
            pltpu.VMEM((NP, D), BF16),
            pltpu.VMEM((128, D), F32),
            pltpu.VMEM((ND, 4, 128), F32),
            pltpu.VMEM((ND, 4, 128), F32),
            pltpu.VMEM((1, 1, 128), I32),
            pltpu.VMEM((ND, 1, 128), I32),
            pltpu.VMEM((3, 64, 128), I32),
            pltpu.VMEM((8, 128), F32),
            pltpu.VMEM((144, 8192), BF16),
            pltpu.VMEM((128, 8192), BF16),
            pltpu.VMEM((16, 4, 2, 4, 4, 8, 128), BF16),
            pltpu.VMEM((16, 8, 128), BF16),
            pltpu.VMEM((D, K1), BF16),
            pltpu.VMEM((D, K1), BF16),
            pltpu.VMEM((NP, 128), F32),
            pltpu.VMEM((1, K1), F32),
            pltpu.VMEM((560, K1), BF16),
            pltpu.VMEM((2, 15, 8, 128), BF16),
            pltpu.SemaphoreType.DMA((8,)),
            pltpu.SemaphoreType.DMA,
            pltpu.SemaphoreType.DMA,
            pltpu.SemaphoreType.DMA,
            pltpu.SemaphoreType.DMA,
            pltpu.SemaphoreType.DMA((8,)),
            pltpu.SemaphoreType.DMA((8,)),
            pltpu.SemaphoreType.DMA((8, 3)),
            pltpu.SemaphoreType.DMA((8, 3)),
            pltpu.SemaphoreType.DMA((8,)),
            pltpu.SemaphoreType.DMA((8,)),
        ],
        compiler_params=pltpu.CompilerParams(
            collective_id=0, has_side_effects=True, vmem_limit_bytes=56 * 1024 * 1024
        ),
    )(
        points, block_rows, block_owner.reshape(-1), block_local, assign_mid.reshape(-1), assign_top.reshape(-1),
    )
    return (lvl1, best.reshape(-1), lvl2, lvl3)


def solution(mesh):
    return jax.shard_map(
        local,
        mesh=mesh,
        in_specs=(
            P(("dp", "group"), None),
            P(("dp", "group")),
            P(("dp", "group"), None),
            P(("dp", "group")),
            P(("dp", "group"), None),
            P("group", None),
        ),
        out_specs=(P(("dp", "group"), None), P(("dp", "group")), P("group", None), P()),
        check_vma=False,
    )
```

```python
import functools

import jax
import jax.numpy as jnp
from jax import lax
from jax.experimental import pallas as pl
from jax.experimental.pallas import tpu as pltpu
from jax.sharding import PartitionSpec as P

MESH = pl.DeviceIdType.MESH
F32 = jnp.float32
BF16 = jnp.bfloat16
I32 = jnp.int32

D = 1024
NB = 64
NP = 8192
ND = 128
K1 = 1024
TM = 2048
NT = (((1,), (1,)), ((), ()))


def wait_for(ref, sem):
    pltpu.make_async_copy(ref, ref, sem).wait()


def iota(shape, dim):
    return lax.broadcasted_iota(I32, shape, dim)


def split2(v):
    hi = v.astype(BF16)
    return hi, (v - hi.astype(F32)).astype(BF16)


def kernel(
    pts, rows_s, own_s, loc_s, mid_s, top_s,
    lvl1, best, lvl2, lvl3,
    xbuf, s2, sendb, recvb, meta, pm, b8, amat, ot, cgh, own_h, wb, rmax, hn, lmsg, rl, lv, tr, l1s, l1r,
    dum63, dum_h,
    xsem, in_s, m1s, m1r, m2s, m2r, bs_s, bs_r, r1, t1, r2, t2, r3, t3,
    v1r, v1s, v2r, v2s, l1_r, l1_s, v3r, v3s,
):
    dp, g = lax.axis_index("dp"), lax.axis_index("group")
    z, core, y, x = dp // 2, dp % 2, g // 4, g % 4

    def turned(v):
        return [v] + [lax.rem(v + a, 4) for a in range(1, 4)]

    zs, cs, ys, xs = turned(z), [core, 1 - core], turned(y), turned(x)
    dps = [[zs[a] * 2 + cs[b] for b in range(2)] for a in range(4)]
    gs = [[ys[a] * 4 + xs[b] for b in range(4)] for a in range(4)]
    dps[0][0], gs[0][0] = dp, g
    lines = [(a, b) for a in range(4) for b in range(2)]
    plane = [(a, b) for a in range(4) for b in range(4)]

    for j in range(8):
        pltpu.make_async_copy(pts.at[pl.ds(1024 * j, 1024)], xbuf.at[pl.ds(1024 * j, 1024)], xsem.at[j]).start()

    barrier = pltpu.get_barrier_semaphore()
    for a, b in lines[1:]:
        pl.semaphore_signal(barrier, inc=1, device_id=(dps[a][b], g), device_id_type=MESH)
    for a, b in plane[1:]:
        pl.semaphore_signal(barrier, inc=1, device_id=(dp, gs[a][b]), device_id_type=MESH)

    lane1 = iota((1, 128), 1)
    m = jnp.zeros((1, 128), I32)
    for b in range(NB):
        m = jnp.where(lane1 == b, (own_s[b] * 8 + loc_s[b]) * 256 + rows_s[b], m)
    for i in range(8):
        m = jnp.where(lane1 == NB + i, mid_s[i], m)
    for i in range(32):
        m = jnp.where(lane1 == NB + 8 + i, top_s[i], m)
    meta[g, dp] = m

    sub8 = iota((8, 1024), 0)
    lane8 = iota((8, 1024), 1)
    in_block = (lane8 // 128) == sub8
    pos = lane8 % 128

    def block_sums(j):
        wait_for(xbuf.at[pl.ds(1024 * j, 1024)], xsem.at[j])
        rv = jnp.zeros((8, 1024), I32)
        for r in range(8):
            rv = jnp.where(sub8 == r, rows_s[8 * j + r], rv)
        mask = jnp.where(in_block & (pos < rv), 1.0, 0.0).astype(BF16)
        s = jnp.dot(mask, xbuf[1024 * j : 1024 * (j + 1), :], preferred_element_type=F32)
        s2[8 * j : 8 * (j + 1), :] = s
        s2[NB + 8 * j : NB + 8 * (j + 1), :] = s

    block_sums(0)
    pl.semaphore_wait(barrier, 22)
    for a, b in lines[1:]:
        pl.semaphore_signal(in_s, inc=1, device_id=(dps[a][b], g), device_id_type=MESH)
    for i, (a, b) in enumerate(lines[1:]):
        pltpu.make_async_remote_copy(
            src_ref=meta.at[g, dp], dst_ref=meta.at[g, dp], send_sem=m1s.at[i], recv_sem=m1r.at[i],
            device_id=(dps[a][b], g), device_id_type=MESH,
        ).start()
    for j in range(1, 4):
        block_sums(j)
    for i, (a, b) in enumerate(lines[1:]):
        wait_for(meta.at[g, dps[(4 - a) % 4][b]], m1r.at[i])
    for a, b in plane[1:]:
        pltpu.make_async_remote_copy(
            src_ref=meta.at[g], dst_ref=meta.at[g], send_sem=m2s, recv_sem=m2r,
            device_id=(dp, gs[a][b]), device_id_type=MESH,
        ).start()
    for j in range(4, 8):
        block_sums(j)
    pl.semaphore_wait(in_s, 7)

    low = iota((16, 8, 128), 2) < 64
    for r, (a, b) in enumerate(lines):
        d = dps[a][b]
        xt = jnp.transpose(s2[:, pl.ds(pl.multiple_of(128 * d, 128), 128)]).reshape(16, 8, 128)
        yt = pltpu.roll(xt, 4, 1)
        sendb[d] = jnp.where(low, xt, yt)[:, 0:4, :]
        for p, q in plane:
            if (a, b, p, q) == (0, 0, 0, 0):
                pltpu.make_async_copy(sendb.at[dp, g], recvb.at[dp, g], bs_r.at[0]).start()
            else:
                pltpu.make_async_remote_copy(
                    src_ref=sendb.at[d, gs[p][q]], dst_ref=recvb.at[dp, g], send_sem=bs_s.at[r], recv_sem=bs_r.at[r],
                    device_id=(d, gs[p][q]), device_id_type=MESH,
                ).start()

    wait_for(meta.at[pl.ds(0, 15)], m2r)
    mt = meta[...].reshape(ND, 128)
    lane64 = iota((64, 128), 1)
    paired = jnp.where(lane64 < 64, mt[0:64], pltpu.roll(mt[64:128], 64, 1))
    owner = paired // 2048
    pm[0] = (owner % 16) * 8 + owner // 16
    pm[1] = (paired // 256) % 8
    pm[2] = paired % 256
    sub128 = iota((128, 128), 0)

    def owners(i, c):
        k = pl.ds(pl.multiple_of(((i % 8) * 8 + i // 8) * 128, 128), 128)
        ot[:, k] = jnp.where(sub128 == pm[0, pl.ds(i, 1), :], 1.0, 0.0).astype(BF16)
        return c

    lax.fori_loop(0, 64, owners, 0, unroll=4)

    low4 = iota((4, 128), 1) < 64
    sub16b = iota((16, 128), 0)
    sums = jnp.zeros((144, 128), F32)
    for r, (a, b) in enumerate(lines):
        d = dps[(4 - a) % 4][b]
        wait_for(recvb.at[d], bs_r.at[r])
        for i in range(8):
            k = pl.ds(pl.multiple_of(d * 1024 + i * 128, 128), 128)
            u, v = recvb[d, i], recvb[d, i + 8]
            b8[i, 0:4, :] = jnp.where(low4, u, pltpu.roll(v, 64, 1))
            b8[i, 4:8, :] = jnp.where(low4, pltpu.roll(u, 64, 1), v)
            hi, mid = split2(b8[i])
            hm = jnp.concatenate([hi.astype(F32), mid.astype(F32)], axis=0)
            row = pl.ds(i * 8 + d, 1)
            loc = pm[1, row, :]
            for l in range(8):
                amat[16 * l : 16 * (l + 1), k] = jnp.where(loc == l, hm, 0.0).astype(BF16)
            cnt = pm[2, row, :].astype(F32)
            amat[128:144, k] = jnp.where(sub16b == loc, cnt, 0.0).astype(BF16)
        ks = pl.ds(pl.multiple_of(d * 1024, 1024), 1024)
        sums = sums + lax.dot_general(amat[:, ks], ot[:, ks], NT, preferred_element_type=F32)
    level1 = []
    for l in range(8):
        c1 = (sums[16 * l : 16 * l + 8] + sums[16 * l + 8 : 16 * l + 16]) / jnp.maximum(sums[128 + l : 129 + l], 1.0)
        level1.append(c1)
        own_h[l // 2, l % 2] = c1.astype(BF16)

    al = slice(None)

    def chunk(ch):
        return cgh.at[ch], own_h.at[ch], dum_h

    def forms(ch):
        if ch % 3 == 0:
            return (
                lambda a, b: (dps[a][0], gs[0][b]),
                (al, core, y, al),
                lambda d: (dp, gs[d][0]),
                lambda d: (al, core, ys[d], al),
            )
        if ch % 3 == 1:
            return (
                lambda a, b: (dp, gs[a][b]),
                (z, core, al, al),
                lambda d: (dps[d][0], g),
                lambda d: (zs[d], core, al, al),
            )
        return (
            lambda a, b: (dps[a][0], gs[b][0]),
            (al, core, al, x),
            lambda d: (dp, gs[0][d]),
            lambda d: (al, core, al, xs[d]),
        )

    def straight(ch):
        buf, src, _ = chunk(ch)
        mine = buf.at[z, core, y, x]
        pltpu.make_async_copy(src, mine, r1.at[ch]).start()
        for a in range(4):
            for p, q in plane:
                if (a, p, q) != (0, 0, 0):
                    pltpu.make_async_remote_copy(
                        src_ref=src, dst_ref=mine, send_sem=t1.at[ch], recv_sem=r1.at[ch],
                        device_id=(dps[a][0], gs[p][q]), device_id_type=MESH,
                    ).start()

    def straight_on(ch):
        buf, _, _ = chunk(ch)
        wait_for(buf.at[:, core], r1.at[ch])
        to_core(ch)

    def to_core(ch):
        buf, _, _ = chunk(ch)
        ref = buf.at[:, core]
        pltpu.make_async_remote_copy(
            src_ref=ref, dst_ref=ref, send_sem=t3.at[ch], recv_sem=r3.at[ch],
            device_id=(dps[0][1], g), device_id_type=MESH,
        ).start()

    def hop1(ch):
        buf, src, _ = chunk(ch)
        peer = forms(ch)[0]
        mine = buf.at[z, core, y, x]
        pltpu.make_async_copy(src, mine, r1.at[ch]).start()
        for a, b in plane[1:]:
            pltpu.make_async_remote_copy(
                src_ref=src, dst_ref=mine, send_sem=t1.at[ch], recv_sem=r1.at[ch],
                device_id=peer(a, b), device_id_type=MESH,
            ).start()

    def hop2(ch):
        buf, _, _ = chunk(ch)
        _, part, peer, _ = forms(ch)
        ref = buf.at[part]
        wait_for(ref, r1.at[ch])
        for d in range(1, 4):
            pltpu.make_async_remote_copy(
                src_ref=ref, dst_ref=ref, send_sem=t2.at[ch, d - 1], recv_sem=r2.at[ch, d - 1],
                device_id=peer(d), device_id_type=MESH,
            ).start()

    def hop3(ch):
        buf, _, _ = chunk(ch)
        part = forms(ch)[3]
        for d in range(1, 4):
            wait_for(buf.at[part(4 - d)], r2.at[ch, d - 1])
        to_core(ch)

    def arrive(ch):
        buf, _, _ = chunk(ch)
        wait_for(buf.at[:, 1 - core], r3.at[ch])
        for l in range(2):
            lanes = slice(256 * ch + 128 * l, 256 * ch + 128 * (l + 1))
            sq = jnp.zeros((8, 128), F32)
            for zz in range(4):
                v = buf[zz, :, :, :, l].astype(F32).reshape(256, 128)
                wb[256 * zz : 256 * (zz + 1), lanes] = v.astype(BF16)
                sq = sq + jnp.sum((v * v).reshape(32, 8, 128), axis=0)
            hn[:, lanes] = 0.5 * jnp.sum(sq, axis=0, keepdims=True)

    def drain(ch):
        buf, _, dum = chunk(ch)
        if ch == 0:
            wait_for(dum63, t1.at[ch])
        else:
            wait_for(dum, t1.at[ch])
            part = forms(ch)[1]
            for d in range(1, 4):
                wait_for(buf.at[part], t2.at[ch, d - 1])
        wait_for(buf.at[:, core], t3.at[ch])

    def upper_levels():
        mtf = meta[...].reshape(ND, 128).astype(F32)
        metat = jnp.transpose(mtf)
        mid_of = jnp.concatenate([metat[NB + l : NB + l + 1, :] for l in range(8)], axis=1).astype(I32)
        member = jnp.where(iota((512, K1), 0) == mid_of, 1.0, 0.0).astype(BF16)
        parts = [split2(c1) for c1 in level1]
        rows = [jnp.concatenate([p[s] for p in parts], axis=1) for s in range(2)]
        both = jnp.concatenate(rows + [jnp.ones((16, K1), BF16)], axis=0)
        got = lax.dot_general(both, member, NT, preferred_element_type=F32)
        level2 = (got[0:8] + got[8:16]) / got[16:24]
        tops = []
        for t in range(4):
            tile = jnp.zeros((1, 128), F32)
            for i in range(4):
                n = (4 * t + i) * 8
                turned_row = pltpu.roll(mtf[n : n + 1, :], (32 * i - NB - 8) % 128, 1)
                tile = jnp.where(lane1 // 32 == i, turned_row, tile)
            tops.append(tile)
        top_of = jnp.concatenate(tops, axis=1).astype(I32)
        member = jnp.where(iota((256, 512), 0) == top_of, 1.0, 0.0).astype(BF16)
        both = jnp.concatenate(list(split2(level2)) + [jnp.ones((16, 512), BF16)], axis=0)
        got = lax.dot_general(both, member, NT, preferred_element_type=F32)
        level3 = (got[0:8] + got[8:16]) / got[16:24]
        part8 = iota((8, 128), 1) // 8
        for n in range(16):
            t = pltpu.roll(level2[:, 128 * (n // 4) : 128 * (n // 4 + 1)], (-32 * (n % 4)) % 128, 1)
            for l in range(8):
                t = jnp.where(part8 == 4 + l, pltpu.roll(level1[l], (32 + 8 * l - 8 * n) % 128, 1), t)
            lmsg[n, 0] = t
            lmsg[n, 1] = level3[:, 0:128]
            lmsg[n, 2] = level3[:, 128:256]
        pltpu.make_async_copy(lmsg.at[g], rl.at[g], v1r).start()
        for a, b in plane[1:]:
            pltpu.make_async_remote_copy(
                src_ref=lmsg.at[gs[a][b]], dst_ref=rl.at[g], send_sem=v1s, recv_sem=v1r,
                device_id=(dp, gs[a][b]), device_id_type=MESH,
            ).start()

    def levels_on_line():
        wait_for(rl, v1r)
        for n in range(2):
            lv[z, core, 128 * n : 128 * (n + 1)] = jnp.transpose(rl[:, n + 1].reshape(128, 128))
        tr[...] = jnp.transpose(rl[:, 0].reshape(128, 128))
        lv[z, core, 256:288] = tr[0:32]
        for n in range(8):
            l1s[n] = tr[pl.ds(32 + n, 8, stride=8), :]
        l1r[dp] = l1s[dp]
        for d in range(1, 4):
            pltpu.make_async_remote_copy(
                src_ref=lv.at[z, core], dst_ref=lv.at[z, core], send_sem=v2s.at[d - 1], recv_sem=v2r.at[d - 1],
                device_id=(dps[d][0], g), device_id_type=MESH,
            ).start()
        for i, (a, b) in enumerate(lines[1:]):
            pltpu.make_async_remote_copy(
                src_ref=l1s.at[dps[a][b]], dst_ref=l1r.at[dp], send_sem=l1_s.at[i], recv_sem=l1_r.at[i],
                device_id=(dps[a][b], g), device_id_type=MESH,
            ).start()

    def levels_to_core():
        for d in range(1, 4):
            wait_for(lv.at[zs[4 - d], core], v2r.at[d - 1])
        pltpu.make_async_remote_copy(
            src_ref=lv.at[:, core], dst_ref=lv.at[:, core], send_sem=v3s, recv_sem=v3r,
            device_id=(dps[0][1], g), device_id_type=MESH,
        ).start()

    def levels_out():
        for i, (a, b) in enumerate(lines[1:]):
            wait_for(l1r.at[dps[(4 - a) % 4][b]], l1_r.at[i])
        wait_for(lv.at[:, 1 - core], v3r)
        for n in range(8):
            lanes = slice(128 * n, 128 * (n + 1))
            lvl3[:, lanes] = lv[n // 2, n % 2, 0:256]
            lvl2[:, lanes] = lv[n // 2, n % 2, 256:288]
            lvl1[:, lanes] = l1r[n]

    def scores(q, lo, hi):
        lanes = slice(256 * q, 256 * (q + 1))

        def tile(t, c):
            rs = pl.ds(pl.multiple_of(t * TM, TM), TM)
            p = jnp.dot(xbuf[rs, :], wb[:, lanes], preferred_element_type=F32) - hn[:, lanes]
            top = jnp.maximum(p[:, 0:128], p[:, 128:256])
            if q > 0:
                top = jnp.maximum(top, rmax[rs, :])
            if q < 3:
                rmax[rs, :] = top
            else:
                for b in range(TM // 128):
                    row = jnp.max(jnp.transpose(top[128 * b : 128 * (b + 1)]), axis=0, keepdims=True)
                    n = t * (TM // 128) + b
                    best[pl.ds(n, 1), :] = jnp.where(lane1 < rows_s[n], row, 0.0 * row)
            return c

        lax.fori_loop(lo, hi, tile, 0)

    straight(0)
    hop1(1)
    hop1(2)
    hop1(3)
    upper_levels()
    straight_on(0)
    hop2(1)
    hop2(2)
    hop2(3)
    levels_on_line()
    arrive(0)
    scores(0, 0, 3)
    hop3(1)
    hop3(2)
    hop3(3)
    scores(0, 3, 4)
    arrive(1)
    scores(1, 0, 4)
    arrive(2)
    levels_to_core()
    scores(2, 0, 4)
    arrive(3)
    scores(3, 0, 4)
    levels_out()

    for i in range(7):
        wait_for(meta.at[g, dp], m1s.at[i])
    wait_for(meta.at[pl.ds(0, 15)], m2s)
    wait_for(sendb.at[0, pl.ds(0, 15)], bs_s.at[0])
    for r in range(1, 8):
        wait_for(sendb.at[0], bs_s.at[r])
    for ch in range(4):
        drain(ch)
    wait_for(rl.at[pl.ds(0, 15)], v1s)
    for d in range(3):
        wait_for(lv.at[0, 0], v2s.at[d])
    for i in range(7):
        wait_for(l1s.at[0], l1_s.at[i])
    wait_for(lv.at[:, core], v3s)


def copies(a, b, c, d, to_a, to_b, to_c, to_d, va, vb, vc, vd, sem, done):
    half = [(d.at[pl.ds(64 * i, 64)], vd.at[pl.ds(64 * i, 64)], to_d.at[pl.ds(64 * i, 64)]) for i in range(4)]
    jobs = half + [(c, vc, to_c), (b, vb, to_b), (a, va, to_a)]
    for i, (x, v, _) in enumerate(jobs):
        pltpu.make_async_copy(x, v, sem.at[i]).start()
    for i, (x, v, y) in enumerate(jobs):
        pltpu.make_async_copy(x, v, sem.at[i]).wait()
        pltpu.make_async_copy(v, y, done.at[i]).start()
    for i, (_, v, y) in enumerate(jobs):
        pltpu.make_async_copy(v, y, done.at[i]).wait()


def local(points, block_rows, block_owner, block_local, assign_mid, assign_top):
    vmem = pl.BlockSpec(memory_space=pltpu.VMEM)
    smem = pl.BlockSpec(memory_space=pltpu.SMEM)
    anywhere = pl.BlockSpec(memory_space=pl.ANY)
    shapes = (
        jax.ShapeDtypeStruct((8, D), F32),
        jax.ShapeDtypeStruct((NB, 128), F32),
        jax.ShapeDtypeStruct((32, D), F32),
        jax.ShapeDtypeStruct((256, D), F32),
    )
    dma = pltpu.SemaphoreType.DMA
    results = pl.pallas_call(
        kernel,
        out_shape=shapes,
        in_specs=[anywhere] + [smem] * 5,
        out_specs=(vmem, vmem, vmem, vmem),
        scratch_shapes=[
            pltpu.VMEM((NP, D), BF16),
            pltpu.VMEM((128, D), F32),
            pltpu.VMEM((8, 16, 4, 128), F32),
            pltpu.VMEM((8, 16, 4, 128), F32),
            pltpu.VMEM((16, 8, 1, 128), I32),
            pltpu.VMEM((3, 64, 128), I32),
            pltpu.VMEM((8, 8, 128), F32),
            pltpu.VMEM((144, 8192), BF16),
            pltpu.VMEM((128, 8192), BF16),
            pltpu.VMEM((4, 4, 2, 4, 4, 2, 8, 128), BF16),
            pltpu.VMEM((4, 2, 8, 128), BF16),
            pltpu.VMEM((D, K1), BF16),
            pltpu.VMEM((NP, 128), F32),
            pltpu.VMEM((1, K1), F32),
            pltpu.VMEM((16, 3, 8, 128), F32),
            pltpu.VMEM((16, 3, 8, 128), F32),
            pltpu.VMEM((4, 2, 288, 128), F32),
            pltpu.VMEM((128, 128), F32),
            pltpu.VMEM((8, 8, 128), F32),
            pltpu.VMEM((8, 8, 128), F32),
            pltpu.VMEM((63, 2, 8, 128), BF16),
            pltpu.VMEM((15, 2, 8, 128), BF16),
            dma((8,)),
            pltpu.SemaphoreType.REGULAR,
            dma((7,)),
            dma((7,)),
            dma,
            dma,
            dma((8,)),
            dma((8,)),
            dma((4,)),
            dma((4,)),
            dma((4, 3)),
            dma((4, 3)),
            dma((4,)),
            dma((4,)),
            dma,
            dma,
            dma((3,)),
            dma((3,)),
            dma((7,)),
            dma((7,)),
            dma,
            dma,
        ],
        compiler_params=pltpu.CompilerParams(
            collective_id=0, has_side_effects=True, vmem_limit_bytes=56 * 1024 * 1024
        ),
    )(
        points, block_rows, block_owner.reshape(-1), block_local, assign_mid.reshape(-1), assign_top.reshape(-1),
    )
    lvl1, best, lvl2, lvl3 = pl.pallas_call(
        copies,
        out_shape=shapes,
        in_specs=[anywhere] * 4,
        out_specs=(anywhere,) * 4,
        scratch_shapes=[pltpu.VMEM(s.shape, F32) for s in shapes] + [dma((7,)), dma((7,))],
    )(*results)
    return (lvl1, best.reshape(-1), lvl2, lvl3)


def solution(mesh):
    return jax.shard_map(
        local,
        mesh=mesh,
        in_specs=(
            P(("dp", "group"), None),
            P(("dp", "group")),
            P(("dp", "group"), None),
            P(("dp", "group")),
            P(("dp", "group"), None),
            P("group", None),
        ),
        out_specs=(P(("dp", "group"), None), P(("dp", "group")), P("group", None), P()),
        check_vma=False,
    )
```

```python
import functools

import jax
import jax.numpy as jnp
from jax import lax
from jax.experimental import pallas as pl
from jax.experimental.pallas import tpu as pltpu
from jax.sharding import PartitionSpec as P

MESH = pl.DeviceIdType.MESH
F32 = jnp.float32
BF16 = jnp.bfloat16
I32 = jnp.int32

D = 1024
NB = 64
NP = 8192
ND = 128
K1 = 1024
TM = 2048
NT = (((1,), (1,)), ((), ()))
STRAIGHT = 2
ORDER = (2, 1, 3, 0)


def wait_for(ref, sem):
    pltpu.make_async_copy(ref, ref, sem).wait()


def iota(shape, dim):
    return lax.broadcasted_iota(I32, shape, dim)


def split2(v):
    hi = v.astype(BF16)
    return hi, (v - hi.astype(F32)).astype(BF16)


def kernel(
    pts, rows_s, own_s, loc_s, mid_s, top_s,
    lvl1, best, lvl2, lvl3,
    xbuf, s2, sendb, recvb, meta, pm, b8, amat, ot, cgh, own_h, wb, rmax, hn, lmsg, rl, lv, tr, l1s, l1r, masks, vb, v1, v2, v3,
    dum63, dum_h, dum127,
    xsem, m2s, m2r, bs_s, bs_r, r1, t1, r2, t2, r3, t3,
    v1r, v1s, v2r, v2s, l1_r, l1_s, v3r, v3s, c0r, c0s, osem,
):
    dp, g = lax.axis_index("dp"), lax.axis_index("group")
    z, core, y, x = dp // 2, dp % 2, g // 4, g % 4

    def turned(v):
        return [v] + [lax.rem(v + a, 4) for a in range(1, 4)]

    zs, cs, ys, xs = turned(z), [core, 1 - core], turned(y), turned(x)
    dps = [[zs[a] * 2 + cs[b] for b in range(2)] for a in range(4)]
    gs = [[ys[a] * 4 + xs[b] for b in range(4)] for a in range(4)]
    dps[0][0], gs[0][0] = dp, g
    lines = [(a, b) for a in range(4) for b in range(2)]
    plane = [(a, b) for a in range(4) for b in range(4)]

    def columns(a):
        return pl.ds(pl.multiple_of(256 * zs[a], 256), 256)

    def load(a):
        pltpu.make_async_copy(pts.at[:, columns(a)], xbuf.at[:, columns(a)], xsem.at[a]).start()

    for a in ORDER[:4]:
        load(a)

    barrier = pltpu.get_barrier_semaphore()
    others = [(a, b, p, q) for a, b in lines for p, q in plane][1:]
    for a, b, p, q in others:
        pl.semaphore_signal(barrier, inc=1, device_id=(dps[a][b], gs[p][q]), device_id_type=MESH)

    lane1 = iota((1, 128), 1)
    m = jnp.zeros((1, 128), I32)
    for b in range(NB):
        m = jnp.where(lane1 == b, (own_s[b] * 8 + loc_s[b]) * 256 + rows_s[b], m)
    for i in range(8):
        m = jnp.where(lane1 == NB + i, mid_s[i], m)
    for i in range(32):
        m = jnp.where(lane1 == NB + 8 + i, top_s[i], m)
    meta[g, dp] = m

    sub8 = iota((8, 1024), 0)
    lane8 = iota((8, 1024), 1)
    in_block = (lane8 // 128) == sub8
    pos = lane8 % 128
    for j in range(8):
        rv = jnp.zeros((8, 1024), I32)
        for r in range(8):
            rv = jnp.where(sub8 == r, rows_s[8 * j + r], rv)
        masks[j] = jnp.where(in_block & (pos < rv), 1.0, 0.0).astype(BF16)

    def block_sums(a):
        wait_for(xbuf.at[:, columns(a)], xsem.at[a])
        for j in range(8):
            t = jnp.dot(masks[j], xbuf[1024 * j : 1024 * (j + 1), columns(a)], preferred_element_type=F32)
            s2[a, 8 * j : 8 * (j + 1), :] = t
            s2[a, NB + 8 * j : NB + 8 * (j + 1), :] = t

    low = iota((16, 8, 128), 2) < 64

    def messages(a):
        for c in range(2):
            xt = jnp.transpose(s2[a, :, 128 * c : 128 * (c + 1)]).reshape(16, 8, 128)
            yt = pltpu.roll(xt, 4, 1)
            sendb[zs[a] * 2 + c] = jnp.where(low, xt, yt)[:, 0:4, :]

    def send_messages(a):
        for b in range(2):
            d = dps[a][b]
            for p, q in plane:
                if (a, b, p, q) == (0, 0, 0, 0):
                    pltpu.make_async_copy(sendb.at[dp, g], recvb.at[dp, g], bs_r.at[0]).start()
                else:
                    pltpu.make_async_remote_copy(
                        src_ref=sendb.at[d, gs[p][q]], dst_ref=recvb.at[dp, g],
                        send_sem=bs_s.at[2 * a + b], recv_sem=bs_r.at[2 * a + b],
                        device_id=(d, gs[p][q]), device_id_type=MESH,
                    ).start()

    pl.semaphore_wait(barrier, ND - 1)
    for a, b, p, q in others:
        pltpu.make_async_remote_copy(
            src_ref=meta.at[g, dp], dst_ref=meta.at[g, dp], send_sem=m2s, recv_sem=m2r,
            device_id=(dps[a][b], gs[p][q]), device_id_type=MESH,
        ).start()
    for k in range(4):
        block_sums(ORDER[k])
        if k + 4 < 4:
            load(ORDER[k + 4])
        messages(ORDER[k])
        send_messages(ORDER[k])

    wait_for(dum127, m2r)
    mt = meta[...].reshape(ND, 128)
    lane64 = iota((64, 128), 1)
    paired = jnp.where(lane64 < 64, mt[0:64], pltpu.roll(mt[64:128], 64, 1))
    owner = paired // 2048
    pm[0] = (owner % 16) * 8 + owner // 16
    pm[1] = (paired // 256) % 8
    pm[2] = paired % 256
    sub128 = iota((128, 128), 0)

    def owners(i, c):
        k = pl.ds(pl.multiple_of(((i % 8) * 8 + i // 8) * 128, 128), 128)
        ot[:, k] = jnp.where(sub128 == pm[0, pl.ds(i, 1), :], 1.0, 0.0).astype(BF16)
        return c

    lax.fori_loop(0, 64, owners, 0, unroll=4)

    low4 = iota((4, 128), 1) < 64
    sub16b = iota((16, 128), 0)
    sums = jnp.zeros((144, 128), F32)
    for a, b in [(a, b) for a in ORDER for b in range(2)]:
        d = dps[(4 - a) % 4][b]
        wait_for(recvb.at[d], bs_r.at[2 * a + b])
        for i in range(8):
            k = pl.ds(pl.multiple_of(d * 1024 + i * 128, 128), 128)
            u, v = recvb[d, i], recvb[d, i + 8]
            b8[i, 0:4, :] = jnp.where(low4, u, pltpu.roll(v, 64, 1))
            b8[i, 4:8, :] = jnp.where(low4, pltpu.roll(u, 64, 1), v)
            hi, mid = split2(b8[i])
            hm = jnp.concatenate([hi.astype(F32), mid.astype(F32)], axis=0)
            row = pl.ds(i * 8 + d, 1)
            loc = pm[1, row, :]
            for l in range(8):
                amat[16 * l : 16 * (l + 1), k] = jnp.where(loc == l, hm, 0.0).astype(BF16)
            cnt = pm[2, row, :].astype(F32)
            amat[128:144, k] = jnp.where(sub16b == loc, cnt, 0.0).astype(BF16)
        ks = pl.ds(pl.multiple_of(d * 1024, 1024), 1024)
        sums = sums + lax.dot_general(amat[:, ks], ot[:, ks], NT, preferred_element_type=F32)
    level1 = []
    for l in range(8):
        c1 = (sums[16 * l : 16 * l + 8] + sums[16 * l + 8 : 16 * l + 16]) / jnp.maximum(sums[128 + l : 129 + l], 1.0)
        level1.append(c1)
        own_h[l // 2, l % 2] = c1.astype(BF16)

    al = slice(None)

    def chunk(ch):
        return cgh.at[ch], own_h.at[ch], dum_h

    def forms(ch):
        if ch % 3 == 0:
            return (
                lambda a, b: (dps[a][0], gs[0][b]),
                (al, core, y, al),
                lambda d: (dp, gs[d][0]),
                lambda d: (al, core, ys[d], al),
            )
        if ch % 3 == 1:
            return (
                lambda a, b: (dp, gs[a][b]),
                (z, core, al, al),
                lambda d: (dps[d][0], g),
                lambda d: (zs[d], core, al, al),
            )
        return (
            lambda a, b: (dps[a][0], gs[b][0]),
            (al, core, al, x),
            lambda d: (dp, gs[0][d]),
            lambda d: (al, core, al, xs[d]),
        )

    def straight(ch):
        buf, src, _ = chunk(ch)
        mine = buf.at[z, core, y, x]
        for a in (2, 1, 3, 0):
            for p, q in plane:
                if (a, p, q) == (0, 0, 0):
                    pltpu.make_async_copy(src, mine, c0r.at[ch, 0]).start()
                else:
                    pltpu.make_async_remote_copy(
                        src_ref=src, dst_ref=mine, send_sem=t1.at[ch], recv_sem=c0r.at[ch, a],
                        device_id=(dps[a][0], gs[p][q]), device_id_type=MESH,
                    ).start()

    def straight_on(ch):
        buf, _, _ = chunk(ch)
        for a in (0, 1, 3, 2):
            ref = buf.at[zs[(4 - a) % 4], core]
            wait_for(ref, c0r.at[ch, a])
            pltpu.make_async_remote_copy(
                src_ref=ref, dst_ref=ref, send_sem=c0s.at[ch, a], recv_sem=c0r.at[ch, 4 + a],
                device_id=(dps[0][1], g), device_id_type=MESH,
            ).start()

    def to_core(ch):
        buf, _, _ = chunk(ch)
        ref = buf.at[:, core]
        pltpu.make_async_remote_copy(
            src_ref=ref, dst_ref=ref, send_sem=t3.at[ch], recv_sem=r3.at[ch],
            device_id=(dps[0][1], g), device_id_type=MESH,
        ).start()

    def hop1(ch):
        buf, src, _ = chunk(ch)
        peer = forms(ch)[0]
        mine = buf.at[z, core, y, x]
        pltpu.make_async_copy(src, mine, r1.at[ch]).start()
        for a, b in plane[1:]:
            pltpu.make_async_remote_copy(
                src_ref=src, dst_ref=mine, send_sem=t1.at[ch], recv_sem=r1.at[ch],
                device_id=peer(a, b), device_id_type=MESH,
            ).start()

    def hop2(ch):
        buf, _, _ = chunk(ch)
        _, part, peer, _ = forms(ch)
        ref = buf.at[part]
        wait_for(ref, r1.at[ch])
        for d in range(1, 4):
            pltpu.make_async_remote_copy(
                src_ref=ref, dst_ref=ref, send_sem=t2.at[ch, d - 1], recv_sem=r2.at[ch, d - 1],
                device_id=peer(d), device_id_type=MESH,
            ).start()

    def hop3(ch):
        buf, _, _ = chunk(ch)
        part = forms(ch)[3]
        for d in range(1, 4):
            wait_for(buf.at[part(4 - d)], r2.at[ch, d - 1])
        to_core(ch)

    def arrive(ch):
        buf, _, _ = chunk(ch)
        if ch < STRAIGHT:
            for a in range(4):
                wait_for(buf.at[zs[(4 - a) % 4], 1 - core], c0r.at[ch, 4 + a])
        else:
            wait_for(buf.at[:, 1 - core], r3.at[ch])
        for l in range(2):
            lanes = slice(256 * ch + 128 * l, 256 * ch + 128 * (l + 1))
            sq = jnp.zeros((8, 128), F32)
            for zz in range(4):
                v = buf[zz, :, :, :, l].astype(F32).reshape(256, 128)
                wb[256 * zz : 256 * (zz + 1), lanes] = v.astype(BF16)
                sq = sq + jnp.sum((v * v).reshape(32, 8, 128), axis=0)
            hn[:, lanes] = 0.5 * jnp.sum(sq, axis=0, keepdims=True)

    def drain(ch):
        buf, _, dum = chunk(ch)
        if ch < STRAIGHT:
            wait_for(dum63, t1.at[ch])
            for a in range(4):
                wait_for(buf.at[0, core], c0s.at[ch, a])
        else:
            wait_for(dum, t1.at[ch])
            part = forms(ch)[1]
            for d in range(1, 4):
                wait_for(buf.at[part], t2.at[ch, d - 1])
            wait_for(buf.at[:, core], t3.at[ch])

    def upper_levels():
        mtf = meta[...].reshape(ND, 128).astype(F32)
        metat = jnp.transpose(mtf)
        mid_of = jnp.concatenate([metat[NB + l : NB + l + 1, :] for l in range(8)], axis=1).astype(I32)
        member = jnp.where(iota((512, K1), 0) == mid_of, 1.0, 0.0).astype(BF16)
        parts = [split2(c1) for c1 in level1]
        rows = [jnp.concatenate([p[s] for p in parts], axis=1) for s in range(2)]
        both = jnp.concatenate(rows + [jnp.ones((16, K1), BF16)], axis=0)
        got = lax.dot_general(both, member, NT, preferred_element_type=F32)
        level2 = (got[0:8] + got[8:16]) / got[16:24]
        tops = []
        for t in range(4):
            tile = jnp.zeros((1, 128), F32)
            for i in range(4):
                n = (4 * t + i) * 8
                turned_row = pltpu.roll(mtf[n : n + 1, :], (32 * i - NB - 8) % 128, 1)
                tile = jnp.where(lane1 // 32 == i, turned_row, tile)
            tops.append(tile)
        top_of = jnp.concatenate(tops, axis=1).astype(I32)
        member = jnp.where(iota((256, 512), 0) == top_of, 1.0, 0.0).astype(BF16)
        both = jnp.concatenate(list(split2(level2)) + [jnp.ones((16, 512), BF16)], axis=0)
        got = lax.dot_general(both, member, NT, preferred_element_type=F32)
        level3 = (got[0:8] + got[8:16]) / got[16:24]
        part8 = iota((8, 128), 1) // 8
        for n in range(16):
            t = pltpu.roll(level2[:, 128 * (n // 4) : 128 * (n // 4 + 1)], (-32 * (n % 4)) % 128, 1)
            for l in range(8):
                t = jnp.where(part8 == 4 + l, pltpu.roll(level1[l], (32 + 8 * l - 8 * n) % 128, 1), t)
            lmsg[n, 0] = t
            lmsg[n, 1] = level3[:, 0:128]
            lmsg[n, 2] = level3[:, 128:256]
        pltpu.make_async_copy(lmsg.at[g], rl.at[g], v1r).start()
        for a, b in plane[1:]:
            pltpu.make_async_remote_copy(
                src_ref=lmsg.at[gs[a][b]], dst_ref=rl.at[g], send_sem=v1s, recv_sem=v1r,
                device_id=(dp, gs[a][b]), device_id_type=MESH,
            ).start()

    def levels_on_line():
        wait_for(rl, v1r)
        for n in range(2):
            lv[z, core, 128 * n : 128 * (n + 1)] = jnp.transpose(rl[:, n + 1].reshape(128, 128))
        tr[...] = jnp.transpose(rl[:, 0].reshape(128, 128))
        lv[z, core, 256:288] = tr[0:32]
        for n in range(8):
            l1s[n] = tr[pl.ds(32 + n, 8, stride=8), :]
        l1r[dp] = l1s[dp]
        for d in range(1, 4):
            pltpu.make_async_remote_copy(
                src_ref=lv.at[z, core], dst_ref=lv.at[z, core], send_sem=v2s.at[d - 1], recv_sem=v2r.at[d - 1],
                device_id=(dps[d][0], g), device_id_type=MESH,
            ).start()
        for i, (a, b) in enumerate(lines[1:]):
            pltpu.make_async_remote_copy(
                src_ref=l1s.at[dps[a][b]], dst_ref=l1r.at[dp], send_sem=l1_s.at[i], recv_sem=l1_r.at[i],
                device_id=(dps[a][b], g), device_id_type=MESH,
            ).start()

    def levels_to_core():
        for d in range(1, 4):
            wait_for(lv.at[zs[4 - d], core], v2r.at[d - 1])
        pltpu.make_async_remote_copy(
            src_ref=lv.at[:, core], dst_ref=lv.at[:, core], send_sem=v3s, recv_sem=v3r,
            device_id=(dps[0][1], g), device_id_type=MESH,
        ).start()

    def levels_out():
        for i, (a, b) in enumerate(lines[1:]):
            wait_for(l1r.at[dps[(4 - a) % 4][b]], l1_r.at[i])
        wait_for(lv.at[:, 1 - core], v3r)
        for n in range(8):
            lanes = slice(128 * n, 128 * (n + 1))
            v3[:, lanes] = lv[n // 2, n % 2, 0:256]
            v2[:, lanes] = lv[n // 2, n % 2, 256:288]
            v1[:, lanes] = l1r[n]
        for i, (v, o) in enumerate(((v1, lvl1), (v2, lvl2), (v3, lvl3))):
            pltpu.make_async_copy(v, o, osem.at[i]).start()

    def scores(q, lo, hi):
        lanes = slice(256 * q, 256 * (q + 1))

        def tile(t, c):
            rs = pl.ds(pl.multiple_of(t * TM, TM), TM)
            p = jnp.dot(xbuf[rs, :], wb[:, lanes], preferred_element_type=F32) - hn[:, lanes]
            top = jnp.maximum(p[:, 0:128], p[:, 128:256])
            if q > 0:
                top = jnp.maximum(top, rmax[rs, :])
            if q < 3:
                rmax[rs, :] = top
            else:
                for b in range(TM // 128):
                    row = jnp.max(jnp.transpose(top[128 * b : 128 * (b + 1)]), axis=0, keepdims=True)
                    n = t * (TM // 128) + b
                    vb[pl.ds(n, 1), :] = jnp.where(lane1 < rows_s[n], row, 0.0 * row)
            return c

        lax.fori_loop(lo, hi, tile, 0)

    straight(0)
    straight(1)
    upper_levels()
    straight_on(0)
    hop1(2)
    hop1(3)
    arrive(0)
    scores(0, 0, 2)
    straight_on(1)
    hop2(2)
    hop2(3)
    scores(0, 2, 4)
    arrive(1)
    levels_on_line()
    scores(1, 0, 2)
    hop3(2)
    hop3(3)
    scores(1, 2, 4)
    arrive(2)
    scores(2, 0, 2)
    levels_to_core()
    scores(2, 2, 4)
    arrive(3)
    levels_out()
    scores(3, 0, 4)
    pltpu.make_async_copy(vb, best, osem.at[3]).start()
    wait_for(dum127, m2s)
    wait_for(sendb.at[0, pl.ds(0, 15)], bs_s.at[0])
    for r in range(1, 8):
        wait_for(sendb.at[0], bs_s.at[r])
    for ch in range(4):
        drain(ch)
    wait_for(rl.at[pl.ds(0, 15)], v1s)
    for d in range(3):
        wait_for(lv.at[0, 0], v2s.at[d])
    for i in range(7):
        wait_for(l1s.at[0], l1_s.at[i])
    wait_for(lv.at[:, core], v3s)
    for i, v in enumerate((v1, v2, v3, vb)):
        wait_for(v, osem.at[i])


def copies(a, b, c, d, to_a, to_b, to_c, to_d, va, vb, vc, vd, sem, done):
    half = [(d.at[pl.ds(64 * i, 64)], vd.at[pl.ds(64 * i, 64)], to_d.at[pl.ds(64 * i, 64)]) for i in range(4)]
    jobs = half + [(c, vc, to_c), (b, vb, to_b), (a, va, to_a)]
    for i, (x, v, _) in enumerate(jobs):
        pltpu.make_async_copy(x, v, sem.at[i]).start()
    for i, (x, v, y) in enumerate(jobs):
        pltpu.make_async_copy(x, v, sem.at[i]).wait()
        pltpu.make_async_copy(v, y, done.at[i]).start()
    for i, (_, v, y) in enumerate(jobs):
        pltpu.make_async_copy(v, y, done.at[i]).wait()


def local(points, block_rows, block_owner, block_local, assign_mid, assign_top):
    smem = pl.BlockSpec(memory_space=pltpu.SMEM)
    anywhere = pl.BlockSpec(memory_space=pl.ANY)
    shapes = (
        jax.ShapeDtypeStruct((8, D), F32),
        jax.ShapeDtypeStruct((NB, 128), F32),
        jax.ShapeDtypeStruct((32, D), F32),
        jax.ShapeDtypeStruct((256, D), F32),
    )
    dma = pltpu.SemaphoreType.DMA
    results = pl.pallas_call(
        kernel,
        out_shape=shapes,
        in_specs=[anywhere] + [smem] * 5,
        out_specs=(anywhere,) * 4,
        scratch_shapes=[
            pltpu.VMEM((NP, D), BF16),
            pltpu.VMEM((4, 128, 256), F32),
            pltpu.VMEM((8, 16, 4, 128), F32),
            pltpu.VMEM((8, 16, 4, 128), F32),
            pltpu.VMEM((16, 8, 1, 128), I32),
            pltpu.VMEM((3, 64, 128), I32),
            pltpu.VMEM((8, 8, 128), F32),
            pltpu.VMEM((144, 8192), BF16),
            pltpu.VMEM((128, 8192), BF16),
            pltpu.VMEM((4, 4, 2, 4, 4, 2, 8, 128), BF16),
            pltpu.VMEM((4, 2, 8, 128), BF16),
            pltpu.VMEM((D, K1), BF16),
            pltpu.VMEM((NP, 128), F32),
            pltpu.VMEM((1, K1), F32),
            pltpu.VMEM((16, 3, 8, 128), F32),
            pltpu.VMEM((16, 3, 8, 128), F32),
            pltpu.VMEM((4, 2, 288, 128), F32),
            pltpu.VMEM((128, 128), F32),
            pltpu.VMEM((8, 8, 128), F32),
            pltpu.VMEM((8, 8, 128), F32),
            pltpu.VMEM((8, 8, 1024), BF16),
            pltpu.VMEM((NB, 128), F32),
            pltpu.VMEM((8, D), F32),
            pltpu.VMEM((32, D), F32),
            pltpu.VMEM((256, D), F32),
            pltpu.VMEM((63, 2, 8, 128), BF16),
            pltpu.VMEM((15, 2, 8, 128), BF16),
            pltpu.VMEM((127, 1, 128), I32),
            dma((4,)),
            dma,
            dma,
            dma((8,)),
            dma((8,)),
            dma((4,)),
            dma((4,)),
            dma((4, 3)),
            dma((4, 3)),
            dma((4,)),
            dma((4,)),
            dma,
            dma,
            dma((3,)),
            dma((3,)),
            dma((7,)),
            dma((7,)),
            dma,
            dma,
            dma((STRAIGHT, 8)),
            dma((STRAIGHT, 4)),
            dma((4,)),
        ],
        compiler_params=pltpu.CompilerParams(
            collective_id=0, has_side_effects=True, vmem_limit_bytes=54 * 1024 * 1024
        ),
    )(
        points, block_rows, block_owner.reshape(-1), block_local, assign_mid.reshape(-1), assign_top.reshape(-1),
    )
    lvl1, best, lvl2, lvl3 = pl.pallas_call(
        copies,
        out_shape=shapes,
        in_specs=[anywhere] * 4,
        out_specs=(anywhere,) * 4,
        scratch_shapes=[pltpu.VMEM(s.shape, F32) for s in shapes] + [dma((7,)), dma((7,))],
    )(*results)
    return (lvl1, best.reshape(-1), lvl2, lvl3)


def solution(mesh):
    return jax.shard_map(
        local,
        mesh=mesh,
        in_specs=(
            P(("dp", "group"), None),
            P(("dp", "group")),
            P(("dp", "group"), None),
            P(("dp", "group")),
            P(("dp", "group"), None),
            P("group", None),
        ),
        out_specs=(P(("dp", "group"), None), P(("dp", "group")), P("group", None), P()),
        check_vma=False,
    )
```

```python
import functools

import jax
import jax.numpy as jnp
from jax import lax
from jax.experimental import pallas as pl
from jax.experimental.pallas import tpu as pltpu
from jax.sharding import PartitionSpec as P

MESH = pl.DeviceIdType.MESH
F32 = jnp.float32
BF16 = jnp.bfloat16
I32 = jnp.int32

D = 1024
NB = 64
NP = 8192
ND = 128
K1 = 1024
TM = 2048
NT = (((1,), (1,)), ((), ()))
STRAIGHT = 2
ORDER = (2, 1, 3, 0)


def wait_for(ref, sem):
    pltpu.make_async_copy(ref, ref, sem).wait()


def iota(shape, dim):
    return lax.broadcasted_iota(I32, shape, dim)


def split2(v):
    hi = v.astype(BF16)
    return hi, (v - hi.astype(F32)).astype(BF16)


def kernel(
    pts, rows_s, own_s, loc_s, mid_s, top_s,
    lvl1, best, lvl2, lvl3,
    xbuf, s2, sendb, recvb, meta, pm, b8, amat, ot, cgh, own_h, wb, rmax, hn, lmsg, rl, lv, tr, l1s, l1r, masks,
    dum63, dum_h, dum127,
    xsem, m2s, m2r, bs_s, bs_r, r1, t1, r2, t2, r3, t3,
    v1r, v1s, v2r, v2s, l1_r, l1_s, v3r, v3s, c0r, c0s,
):
    dp, g = lax.axis_index("dp"), lax.axis_index("group")
    z, core, y, x = dp // 2, dp % 2, g // 4, g % 4

    def turned(v):
        return [v] + [lax.rem(v + a, 4) for a in range(1, 4)]

    zs, cs, ys, xs = turned(z), [core, 1 - core], turned(y), turned(x)
    dps = [[zs[a] * 2 + cs[b] for b in range(2)] for a in range(4)]
    gs = [[ys[a] * 4 + xs[b] for b in range(4)] for a in range(4)]
    dps[0][0], gs[0][0] = dp, g
    lines = [(a, b) for a in range(4) for b in range(2)]
    plane = [(a, b) for a in range(4) for b in range(4)]

    def columns(a):
        return pl.ds(pl.multiple_of(256 * zs[a], 256), 256)

    def load(a):
        pltpu.make_async_copy(pts.at[:, columns(a)], xbuf.at[:, columns(a)], xsem.at[a]).start()

    for a in ORDER[:4]:
        load(a)

    barrier = pltpu.get_barrier_semaphore()
    others = [(a, b, p, q) for a, b in lines for p, q in plane][1:]
    for a, b, p, q in others:
        pl.semaphore_signal(barrier, inc=1, device_id=(dps[a][b], gs[p][q]), device_id_type=MESH)

    lane1 = iota((1, 128), 1)
    m = jnp.zeros((1, 128), I32)
    for b in range(NB):
        m = jnp.where(lane1 == b, (own_s[b] * 8 + loc_s[b]) * 256 + rows_s[b], m)
    for i in range(8):
        m = jnp.where(lane1 == NB + i, mid_s[i], m)
    for i in range(32):
        m = jnp.where(lane1 == NB + 8 + i, top_s[i], m)
    meta[g, dp] = m

    sub8 = iota((8, 1024), 0)
    lane8 = iota((8, 1024), 1)
    in_block = (lane8 // 128) == sub8
    pos = lane8 % 128
    for j in range(8):
        rv = jnp.zeros((8, 1024), I32)
        for r in range(8):
            rv = jnp.where(sub8 == r, rows_s[8 * j + r], rv)
        masks[j] = jnp.where(in_block & (pos < rv), 1.0, 0.0).astype(BF16)

    def block_sums(a):
        wait_for(xbuf.at[:, columns(a)], xsem.at[a])
        for j in range(8):
            t = jnp.dot(masks[j], xbuf[1024 * j : 1024 * (j + 1), columns(a)], preferred_element_type=F32)
            s2[a, 8 * j : 8 * (j + 1), :] = t
            s2[a, NB + 8 * j : NB + 8 * (j + 1), :] = t

    low = iota((16, 8, 128), 2) < 64

    def messages(a):
        for c in range(2):
            xt = jnp.transpose(s2[a, :, 128 * c : 128 * (c + 1)]).reshape(16, 8, 128)
            yt = pltpu.roll(xt, 4, 1)
            sendb[zs[a] * 2 + c] = jnp.where(low, xt, yt)[:, 0:4, :]

    def send_messages(a):
        for b in range(2):
            d = dps[a][b]
            for p, q in plane:
                if (a, b, p, q) == (0, 0, 0, 0):
                    pltpu.make_async_copy(sendb.at[dp, g], recvb.at[dp, g], bs_r.at[0]).start()
                else:
                    pltpu.make_async_remote_copy(
                        src_ref=sendb.at[d, gs[p][q]], dst_ref=recvb.at[dp, g],
                        send_sem=bs_s.at[2 * a + b], recv_sem=bs_r.at[2 * a + b],
                        device_id=(d, gs[p][q]), device_id_type=MESH,
                    ).start()

    pl.semaphore_wait(barrier, ND - 1)
    for a, b, p, q in others:
        pltpu.make_async_remote_copy(
            src_ref=meta.at[g, dp], dst_ref=meta.at[g, dp], send_sem=m2s, recv_sem=m2r,
            device_id=(dps[a][b], gs[p][q]), device_id_type=MESH,
        ).start()
    for k in range(4):
        block_sums(ORDER[k])
        if k + 4 < 4:
            load(ORDER[k + 4])
        messages(ORDER[k])
        send_messages(ORDER[k])

    wait_for(dum127, m2r)
    mt = meta[...].reshape(ND, 128)
    lane64 = iota((64, 128), 1)
    paired = jnp.where(lane64 < 64, mt[0:64], pltpu.roll(mt[64:128], 64, 1))
    owner = paired // 2048
    pm[0] = (owner % 16) * 8 + owner // 16
    pm[1] = (paired // 256) % 8
    pm[2] = paired % 256
    sub128 = iota((128, 128), 0)

    def owners(i, c):
        k = pl.ds(pl.multiple_of(((i % 8) * 8 + i // 8) * 128, 128), 128)
        ot[:, k] = jnp.where(sub128 == pm[0, pl.ds(i, 1), :], 1.0, 0.0).astype(BF16)
        return c

    lax.fori_loop(0, 64, owners, 0, unroll=4)

    low4 = iota((4, 128), 1) < 64
    sub16b = iota((16, 128), 0)
    sums = jnp.zeros((144, 128), F32)
    for a, b in [(a, b) for a in ORDER for b in range(2)]:
        d = dps[(4 - a) % 4][b]
        wait_for(recvb.at[d], bs_r.at[2 * a + b])
        for i in range(8):
            k = pl.ds(pl.multiple_of(d * 1024 + i * 128, 128), 128)
            u, v = recvb[d, i], recvb[d, i + 8]
            b8[i, 0:4, :] = jnp.where(low4, u, pltpu.roll(v, 64, 1))
            b8[i, 4:8, :] = jnp.where(low4, pltpu.roll(u, 64, 1), v)
            hi, mid = split2(b8[i])
            hm = jnp.concatenate([hi.astype(F32), mid.astype(F32)], axis=0)
            row = pl.ds(i * 8 + d, 1)
            loc = pm[1, row, :]
            for l in range(8):
                amat[16 * l : 16 * (l + 1), k] = jnp.where(loc == l, hm, 0.0).astype(BF16)
            cnt = pm[2, row, :].astype(F32)
            amat[128:144, k] = jnp.where(sub16b == loc, cnt, 0.0).astype(BF16)
        ks = pl.ds(pl.multiple_of(d * 1024, 1024), 1024)
        sums = sums + lax.dot_general(amat[:, ks], ot[:, ks], NT, preferred_element_type=F32)
    level1 = []
    for l in range(8):
        c1 = (sums[16 * l : 16 * l + 8] + sums[16 * l + 8 : 16 * l + 16]) / jnp.maximum(sums[128 + l : 129 + l], 1.0)
        level1.append(c1)
        own_h[l // 2, l % 2] = c1.astype(BF16)

    al = slice(None)

    def chunk(ch):
        return cgh.at[ch], own_h.at[ch], dum_h

    def forms(ch):
        if ch % 3 == 0:
            return (
                lambda a, b: (dps[a][0], gs[0][b]),
                (al, core, y, al),
                lambda d: (dp, gs[d][0]),
                lambda d: (al, core, ys[d], al),
            )
        if ch % 3 == 1:
            return (
                lambda a, b: (dp, gs[a][b]),
                (z, core, al, al),
                lambda d: (dps[d][0], g),
                lambda d: (zs[d], core, al, al),
            )
        return (
            lambda a, b: (dps[a][0], gs[b][0]),
            (al, core, al, x),
            lambda d: (dp, gs[0][d]),
            lambda d: (al, core, al, xs[d]),
        )

    def straight(ch):
        buf, src, _ = chunk(ch)
        mine = buf.at[z, core, y, x]
        for a in (2, 1, 3, 0):
            for p, q in plane:
                if (a, p, q) == (0, 0, 0):
                    pltpu.make_async_copy(src, mine, c0r.at[ch, 0]).start()
                else:
                    pltpu.make_async_remote_copy(
                        src_ref=src, dst_ref=mine, send_sem=t1.at[ch], recv_sem=c0r.at[ch, a],
                        device_id=(dps[a][0], gs[p][q]), device_id_type=MESH,
                    ).start()

    def straight_on(ch):
        buf, _, _ = chunk(ch)
        for a in (0, 1, 3, 2):
            ref = buf.at[zs[(4 - a) % 4], core]
            wait_for(ref, c0r.at[ch, a])
            pltpu.make_async_remote_copy(
                src_ref=ref, dst_ref=ref, send_sem=c0s.at[ch, a], recv_sem=c0r.at[ch, 4 + a],
                device_id=(dps[0][1], g), device_id_type=MESH,
            ).start()

    def to_core(ch):
        buf, _, _ = chunk(ch)
        ref = buf.at[:, core]
        pltpu.make_async_remote_copy(
            src_ref=ref, dst_ref=ref, send_sem=t3.at[ch], recv_sem=r3.at[ch],
            device_id=(dps[0][1], g), device_id_type=MESH,
        ).start()

    def hop1(ch):
        buf, src, _ = chunk(ch)
        peer = forms(ch)[0]
        mine = buf.at[z, core, y, x]
        pltpu.make_async_copy(src, mine, r1.at[ch]).start()
        for a, b in plane[1:]:
            pltpu.make_async_remote_copy(
                src_ref=src, dst_ref=mine, send_sem=t1.at[ch], recv_sem=r1.at[ch],
                device_id=peer(a, b), device_id_type=MESH,
            ).start()

    def hop2(ch):
        buf, _, _ = chunk(ch)
        _, part, peer, _ = forms(ch)
        ref = buf.at[part]
        wait_for(ref, r1.at[ch])
        for d in range(1, 4):
            pltpu.make_async_remote_copy(
                src_ref=ref, dst_ref=ref, send_sem=t2.at[ch, d - 1], recv_sem=r2.at[ch, d - 1],
                device_id=peer(d), device_id_type=MESH,
            ).start()

    def hop3(ch):
        buf, _, _ = chunk(ch)
        part = forms(ch)[3]
        for d in range(1, 4):
            wait_for(buf.at[part(4 - d)], r2.at[ch, d - 1])
        to_core(ch)

    def arrive(ch):
        buf, _, _ = chunk(ch)
        if ch < STRAIGHT:
            for a in range(4):
                wait_for(buf.at[zs[(4 - a) % 4], 1 - core], c0r.at[ch, 4 + a])
        else:
            wait_for(buf.at[:, 1 - core], r3.at[ch])
        for l in range(2):
            lanes = slice(256 * ch + 128 * l, 256 * ch + 128 * (l + 1))
            sq = jnp.zeros((8, 128), F32)
            for zz in range(4):
                v = buf[zz, :, :, :, l].astype(F32).reshape(256, 128)
                wb[256 * zz : 256 * (zz + 1), lanes] = v.astype(BF16)
                sq = sq + jnp.sum((v * v).reshape(32, 8, 128), axis=0)
            hn[:, lanes] = 0.5 * jnp.sum(sq, axis=0, keepdims=True)

    def drain(ch):
        buf, _, dum = chunk(ch)
        if ch < STRAIGHT:
            wait_for(dum63, t1.at[ch])
            for a in range(4):
                wait_for(buf.at[0, core], c0s.at[ch, a])
        else:
            wait_for(dum, t1.at[ch])
            part = forms(ch)[1]
            for d in range(1, 4):
                wait_for(buf.at[part], t2.at[ch, d - 1])
            wait_for(buf.at[:, core], t3.at[ch])

    def upper_levels():
        mtf = meta[...].reshape(ND, 128).astype(F32)
        metat = jnp.transpose(mtf)
        mid_of = jnp.concatenate([metat[NB + l : NB + l + 1, :] for l in range(8)], axis=1).astype(I32)
        member = jnp.where(iota((512, K1), 0) == mid_of, 1.0, 0.0).astype(BF16)
        parts = [split2(c1) for c1 in level1]
        rows = [jnp.concatenate([p[s] for p in parts], axis=1) for s in range(2)]
        both = jnp.concatenate(rows + [jnp.ones((16, K1), BF16)], axis=0)
        got = lax.dot_general(both, member, NT, preferred_element_type=F32)
        level2 = (got[0:8] + got[8:16]) / got[16:24]
        tops = []
        for t in range(4):
            tile = jnp.zeros((1, 128), F32)
            for i in range(4):
                n = (4 * t + i) * 8
                turned_row = pltpu.roll(mtf[n : n + 1, :], (32 * i - NB - 8) % 128, 1)
                tile = jnp.where(lane1 // 32 == i, turned_row, tile)
            tops.append(tile)
        top_of = jnp.concatenate(tops, axis=1).astype(I32)
        member = jnp.where(iota((256, 512), 0) == top_of, 1.0, 0.0).astype(BF16)
        both = jnp.concatenate(list(split2(level2)) + [jnp.ones((16, 512), BF16)], axis=0)
        got = lax.dot_general(both, member, NT, preferred_element_type=F32)
        level3 = (got[0:8] + got[8:16]) / got[16:24]
        part8 = iota((8, 128), 1) // 8
        for n in range(16):
            t = pltpu.roll(level2[:, 128 * (n // 4) : 128 * (n // 4 + 1)], (-32 * (n % 4)) % 128, 1)
            for l in range(8):
                t = jnp.where(part8 == 4 + l, pltpu.roll(level1[l], (32 + 8 * l - 8 * n) % 128, 1), t)
            lmsg[n, 0] = t
            lmsg[n, 1] = level3[:, 0:128]
            lmsg[n, 2] = level3[:, 128:256]
        pltpu.make_async_copy(lmsg.at[g], rl.at[g], v1r).start()
        for a, b in plane[1:]:
            pltpu.make_async_remote_copy(
                src_ref=lmsg.at[gs[a][b]], dst_ref=rl.at[g], send_sem=v1s, recv_sem=v1r,
                device_id=(dp, gs[a][b]), device_id_type=MESH,
            ).start()

    def levels_on_line():
        wait_for(rl, v1r)
        for n in range(2):
            lv[z, core, 128 * n : 128 * (n + 1)] = jnp.transpose(rl[:, n + 1].reshape(128, 128))
        tr[...] = jnp.transpose(rl[:, 0].reshape(128, 128))
        lv[z, core, 256:288] = tr[0:32]
        for n in range(8):
            l1s[n] = tr[pl.ds(32 + n, 8, stride=8), :]
        l1r[dp] = l1s[dp]
        for d in range(1, 4):
            pltpu.make_async_remote_copy(
                src_ref=lv.at[z, core], dst_ref=lv.at[z, core], send_sem=v2s.at[d - 1], recv_sem=v2r.at[d - 1],
                device_id=(dps[d][0], g), device_id_type=MESH,
            ).start()
        for i, (a, b) in enumerate(lines[1:]):
            pltpu.make_async_remote_copy(
                src_ref=l1s.at[dps[a][b]], dst_ref=l1r.at[dp], send_sem=l1_s.at[i], recv_sem=l1_r.at[i],
                device_id=(dps[a][b], g), device_id_type=MESH,
            ).start()

    def levels_to_core():
        for d in range(1, 4):
            wait_for(lv.at[zs[4 - d], core], v2r.at[d - 1])
        pltpu.make_async_remote_copy(
            src_ref=lv.at[:, core], dst_ref=lv.at[:, core], send_sem=v3s, recv_sem=v3r,
            device_id=(dps[0][1], g), device_id_type=MESH,
        ).start()

    def levels_out():
        for i, (a, b) in enumerate(lines[1:]):
            wait_for(l1r.at[dps[(4 - a) % 4][b]], l1_r.at[i])
        wait_for(lv.at[:, 1 - core], v3r)
        for n in range(8):
            lanes = slice(128 * n, 128 * (n + 1))
            lvl3[:, lanes] = lv[n // 2, n % 2, 0:256]
            lvl2[:, lanes] = lv[n // 2, n % 2, 256:288]
            lvl1[:, lanes] = l1r[n]

    def scores(q, lo, hi):
        lanes = slice(256 * q, 256 * (q + 1))

        def tile(t, c):
            rs = pl.ds(pl.multiple_of(t * TM, TM), TM)
            p = jnp.dot(xbuf[rs, :], wb[:, lanes], preferred_element_type=F32) - hn[:, lanes]
            top = jnp.maximum(p[:, 0:128], p[:, 128:256])
            if q > 0:
                top = jnp.maximum(top, rmax[rs, :])
            if q < 3:
                rmax[rs, :] = top
            else:
                for b in range(TM // 128):
                    row = jnp.max(jnp.transpose(top[128 * b : 128 * (b + 1)]), axis=0, keepdims=True)
                    n = t * (TM // 128) + b
                    best[pl.ds(n, 1), :] = jnp.where(lane1 < rows_s[n], row, 0.0 * row)
            return c

        lax.fori_loop(lo, hi, tile, 0)

    straight(0)
    straight(1)
    upper_levels()
    straight_on(0)
    hop1(2)
    hop1(3)
    arrive(0)
    scores(0, 0, 2)
    straight_on(1)
    hop2(2)
    hop2(3)
    scores(0, 2, 4)
    arrive(1)
    levels_on_line()
    scores(1, 0, 2)
    hop3(2)
    hop3(3)
    scores(1, 2, 4)
    arrive(2)
    scores(2, 0, 2)
    levels_to_core()
    scores(2, 2, 4)
    arrive(3)
    levels_out()
    scores(3, 0, 4)
    wait_for(dum127, m2s)
    wait_for(sendb.at[0, pl.ds(0, 15)], bs_s.at[0])
    for r in range(1, 8):
        wait_for(sendb.at[0], bs_s.at[r])
    for ch in range(4):
        drain(ch)
    wait_for(rl.at[pl.ds(0, 15)], v1s)
    for d in range(3):
        wait_for(lv.at[0, 0], v2s.at[d])
    for i in range(7):
        wait_for(l1s.at[0], l1_s.at[i])
    wait_for(lv.at[:, core], v3s)


def copies(*refs):
    for i in range(4):
        pltpu.make_async_copy(refs[i], refs[4 + i], refs[8].at[i]).start()
    for i in range(4):
        pltpu.make_async_copy(refs[i], refs[4 + i], refs[8].at[i]).wait()


def local(points, block_rows, block_owner, block_local, assign_mid, assign_top):
    smem = pl.BlockSpec(memory_space=pltpu.SMEM)
    anywhere = pl.BlockSpec(memory_space=pl.ANY)
    vmem = pl.BlockSpec(memory_space=pltpu.VMEM)
    shapes = (
        jax.ShapeDtypeStruct((8, D), F32),
        jax.ShapeDtypeStruct((NB, 128), F32),
        jax.ShapeDtypeStruct((32, D), F32),
        jax.ShapeDtypeStruct((256, D), F32),
    )
    dma = pltpu.SemaphoreType.DMA
    results = pl.pallas_call(
        kernel,
        out_shape=tuple(pltpu.VMEM(s.shape, F32) for s in shapes),
        in_specs=[anywhere] + [smem] * 5,
        out_specs=(vmem,) * 4,
        scratch_shapes=[
            pltpu.VMEM((NP, D), BF16),
            pltpu.VMEM((4, 128, 256), F32),
            pltpu.VMEM((8, 16, 4, 128), F32),
            pltpu.VMEM((8, 16, 4, 128), F32),
            pltpu.VMEM((16, 8, 1, 128), I32),
            pltpu.VMEM((3, 64, 128), I32),
            pltpu.VMEM((8, 8, 128), F32),
            pltpu.VMEM((144, 8192), BF16),
            pltpu.VMEM((128, 8192), BF16),
            pltpu.VMEM((4, 4, 2, 4, 4, 2, 8, 128), BF16),
            pltpu.VMEM((4, 2, 8, 128), BF16),
            pltpu.VMEM((D, K1), BF16),
            pltpu.VMEM((NP, 128), F32),
            pltpu.VMEM((1, K1), F32),
            pltpu.VMEM((16, 3, 8, 128), F32),
            pltpu.VMEM((16, 3, 8, 128), F32),
            pltpu.VMEM((4, 2, 288, 128), F32),
            pltpu.VMEM((128, 128), F32),
            pltpu.VMEM((8, 8, 128), F32),
            pltpu.VMEM((8, 8, 128), F32),
            pltpu.VMEM((8, 8, 1024), BF16),
            pltpu.VMEM((63, 2, 8, 128), BF16),
            pltpu.VMEM((15, 2, 8, 128), BF16),
            pltpu.VMEM((127, 1, 128), I32),
            dma((4,)),
            dma,
            dma,
            dma((8,)),
            dma((8,)),
            dma((4,)),
            dma((4,)),
            dma((4, 3)),
            dma((4, 3)),
            dma((4,)),
            dma((4,)),
            dma,
            dma,
            dma((3,)),
            dma((3,)),
            dma((7,)),
            dma((7,)),
            dma,
            dma,
            dma((STRAIGHT, 8)),
            dma((STRAIGHT, 4)),
        ],
        compiler_params=pltpu.CompilerParams(
            collective_id=0, has_side_effects=True, vmem_limit_bytes=54 * 1024 * 1024
        ),
    )(
        points, block_rows, block_owner.reshape(-1), block_local, assign_mid.reshape(-1), assign_top.reshape(-1),
    )
    lvl1, best, lvl2, lvl3 = pl.pallas_call(
        copies,
        out_shape=shapes,
        in_specs=[vmem] * 4,
        out_specs=(anywhere,) * 4,
        scratch_shapes=[dma((4,))],
    )(*[pltpu.with_memory_space_constraint(r, pltpu.VMEM) for r in results])
    return (lvl1, best.reshape(-1), lvl2, lvl3)


def solution(mesh):
    return jax.shard_map(
        local,
        mesh=mesh,
        in_specs=(
            P(("dp", "group"), None),
            P(("dp", "group")),
            P(("dp", "group"), None),
            P(("dp", "group")),
            P(("dp", "group"), None),
            P("group", None),
        ),
        out_specs=(P(("dp", "group"), None), P(("dp", "group")), P("group", None), P()),
        check_vma=False,
    )
```
